32 devices in a mesh: grp: 4 (over y, core), seq: 8 (over z, x).
Axes of the slice: x: 2, y: 2, z: 4, core: 2. Of those that a mesh axis runs over, the one named last changes fastest.
Arguments:
- tokens: bfloat16 [4, 2048, 2048], P('grp', 'seq'), may hold values from -6 to 6
- cotangent: bfloat16 [4, 2048, 2048], P('grp', 'seq'), may hold values from -6 to 6
- route_ids: int32 [4, 2048, 8], P('grp', 'seq'), may hold values from 0 to 15, all different within a row; in each aligned block of 256 rows (0 to 255, 256 to 511, ..., all dimensions but the last counted through in order) at most 144 rows name the same one
- gain_attn: bfloat16 [2048], P(('grp', 'seq')), may hold values from 0.099609375 to 1.8984375
- w_query: bfloat16 [2048, 2048], P(('grp', 'seq')), may hold values from -0.125 to 0.125
- w_key: bfloat16 [2048, 2048], P(('grp', 'seq')), may hold values from -0.125 to 0.125
- w_value: bfloat16 [2048, 2048], P(('grp', 'seq')), may hold values from -0.125 to 0.125
- w_out: bfloat16 [2048, 2048], P(('grp', 'seq')), may hold values from -1.5 to 1.5
- gain_query: bfloat16 [2048], P(('grp', 'seq')), may hold values from 0.099609375 to 1.8984375
- gain_key: bfloat16 [2048], P(('grp', 'seq')), may hold values from 0.099609375 to 1.8984375
- gain_ffn: bfloat16 [2048], P(('grp', 'seq')), may hold values from 0.099609375 to 1.8984375
- router: bfloat16 [2048, 16], P(('grp', 'seq')), may hold values from -0.125 to 0.125
- expert_gate: bfloat16 [16, 2048, 1024], P('seq', 'grp'), may hold values from -0.125 to 0.125
- expert_up: bfloat16 [16, 2048, 1024], P('seq', 'grp'), may hold values from -0.125 to 0.125
- expert_down: bfloat16 [16, 1024, 2048], P('seq', 'grp'), may hold values from -1.5 to 1.5
- clip_flags: int32 [16], replicated, may hold values from 0 to 1
- clip_factors: float32 [16], replicated, may hold values from 0.25 to 1
Outputs:
- block_out: bfloat16 [4, 2048, 2048], P('grp', 'seq')
- tokens_grad: float32 [4, 2048, 2048], P('grp', 'seq')
- gain_attn_grad: float32 [2048], P(('grp', 'seq'))
- w_query_grad: float32 [2048, 2048], P(('grp', 'seq'))
- w_key_grad: float32 [2048, 2048], P(('grp', 'seq'))
- w_value_grad: float32 [2048, 2048], P(('grp', 'seq'))
- w_out_grad: float32 [2048, 2048], P(('grp', 'seq'))
- gain_query_grad: float32 [2048], P(('grp', 'seq'))
- gain_key_grad: float32 [2048], P(('grp', 'seq'))
- gain_ffn_grad: float32 [2048], P(('grp', 'seq'))
- router_grad: float32 [2048, 16], P(('grp', 'seq'))
- expert_gate_grad: float32 [16, 2048, 1024], P('seq', 'grp')
- expert_up_grad: float32 [16, 2048, 1024], P('seq', 'grp')
- expert_down_grad: float32 [16, 1024, 2048], P('seq', 'grp')
- max_logit: float32 [16], replicated
- clipped_query: bfloat16 [2048, 2048], P(('grp', 'seq'))
- clipped_key: bfloat16 [2048, 2048], P(('grp', 'seq'))
The draws below stay inside these ranges and needn't reach their ends.
Inputs may be any that keep to these rules, and one draw needn't show every extreme that they name: `route_ids`: each row names 8 different experts. In every aligned block of 256 rows of one group (the rows of one group on one index of seq) no expert is named by more than 144 rows, and in some blocks one expert is named by exactly 144 rows.
All inputs are finite; a program needn't handle non-finite values.
Results may differ from the reference program's by a relative error of at most 0.023.
Values may be sent and summed in bfloat16 or wider, within the bound.
A program may use at most 384 MiB of HBM per device.

```python
import math
from functools import partial
import jax
import jax.numpy as jnp
import numpy as np
from jax import lax

D = 2048
H = 16
HD = 128
FF = 1024
TOP = 8
E = 16
PROMPT = 1024
CONT_LEN = 128
GROUP_TOK = 2048
GROUPS = 4
ROWS = 256
CAP_G = 144
N_SEQ = 8


def place_ends(values, own_key, smallest, largest):
    longest = values.shape.index(max(values.shape))
    spots = []
    for shift in (0, 1):
        where = [jax.random.randint(jax.random.fold_in(own_key, axis), (), 0, length) for axis, length in enumerate(values.shape)]
        where[longest] = (where[longest] + shift) % values.shape[longest]
        spots.append(tuple(where))
    return values.at[spots[0]].set(smallest).at[spots[1]].set(largest)


def block_levels(stream_key, extent, cuts, least, high):
    level = 1.0
    for axis_at, shards_of in cuts:
        heights = jax.random.uniform(jax.random.fold_in(jax.random.fold_in(stream_key, 6), axis_at), (shards_of,), jnp.float32, least / len(cuts), high / len(cuts))
        level = level * jnp.repeat(jnp.exp(heights), extent[axis_at] // shards_of).reshape((-1,) + (1,) * (len(extent) - 1 - axis_at))
    return level


def assign_block(rng, own, number, rows, amount, top, reach, lean):
    sequence = jax.random.permutation(rng, amount)
    crowded, usual = load_shares(amount, rows * top, reach, lean, True), load_shares(amount, rows * top, reach, lean, False)
    places = jnp.arange(amount)

    def named(tallies, turn):
        used = int((tallies > 0).sum())
        fixed = max(1, used // 4)
        shifted = fixed + (places - fixed + turn * (used - fixed)) % max(1, amount - fixed)
        return jnp.zeros((amount,), jnp.int32).at[sequence[jnp.where(places < fixed, places, shifted)]].set(jnp.asarray(tallies, jnp.int32))

    tallies = jnp.where(number % 4 == 0, named(crowded, number // 4), named(usual, number - number // 4 - 1))
    mixed = jax.random.permutation(jax.random.fold_in(own, 3), amount)
    source_of, receiver = mixed[0:amount // 2 * 2:2], mixed[1:amount // 2 * 2:2]
    room = jnp.minimum(tallies[source_of] - 1, reach - tallies[receiver]) // 2
    room = jnp.where((source_of == sequence[0]) | (receiver == sequence[0]) | (tallies[receiver] == 0), 0, jnp.maximum(room, 0))
    shifted = jax.random.randint(jax.random.fold_in(own, 4), (amount // 2,), 0, 1 << 20) % (room + 1)
    tallies = tallies.at[source_of].add(-shifted).at[receiver].add(shifted)
    items = jnp.searchsorted(jnp.cumsum(tallies), jnp.arange(rows * top), side="right").astype(jnp.int32)
    grid = items.reshape(top, rows).T
    grid = grid[jax.random.permutation(jax.random.fold_in(own, 1), rows)]
    turn = jax.random.randint(jax.random.fold_in(own, 2), (rows, 1), 0, top)
    return jnp.take_along_axis(grid, (jnp.arange(top)[None, :] + turn) % top, axis=1)


def load_shares(number_of, total, bound, skew, full):
    portions = [(1 << 20) // math.isqrt(grade ** skew) + 1 for grade in range(1, number_of + 1)]
    largest = bound if full else min(bound, max(-(-total // number_of), total * portions[0] // sum(portions)))
    least = 1 if total - largest >= number_of - 1 else 0
    holding, rest = [largest] + [least] * (number_of - 1), total - largest - least * (number_of - 1)
    while rest > 0:
        candidates = [i for i in range(1, number_of) if holding[i] < largest] or [i for i in range(1, number_of) if holding[i] < bound]
        pool, budget = sum([portions[i] for i in candidates]), rest
        for i in candidates:
            extra = min(bound - holding[i], max(1, budget * portions[i] // pool), rest)
            holding[i] = holding[i] + extra
            rest = rest - extra
    return np.array(holding)


def gaussian(key, extent, width, limit, shards=(), held_as=jnp.bfloat16):
    values = jax.random.normal(key, extent, jnp.float32) * width
    if len(shards) > 0:
        values = block_levels(key, extent, shards, -0.22, 0.18) * values
    return jnp.clip(values, min=-limit, max=limit).astype(held_as)


def setup_inputs(seed: int = 0) -> dict:
    splits = jax.random.split(jax.random.key(seed), 18)
    tokens = gaussian(splits[0], (GROUPS, GROUP_TOK, D), 1.0, 6.0, ((0, 4), (1, 8)))
    cotangent = gaussian(splits[1], (GROUPS, GROUP_TOK, D), 1.0, 6.0, ((0, 4), (1, 8)))
    route_ids_keys = jax.random.split(jax.random.fold_in(splits[2], 1), GROUPS * GROUP_TOK // ROWS)
    route_ids_turns = jax.random.permutation(jax.random.fold_in(splits[2], 3), GROUPS * GROUP_TOK // ROWS)
    route_ids = jax.vmap(lambda own, number: assign_block(jax.random.fold_in(splits[2], 2), own, number, ROWS, E, TOP, CAP_G, 0))(route_ids_keys, route_ids_turns).reshape((GROUPS, GROUP_TOK, TOP))
    gain_attn = jnp.clip(1.0 + 0.18 * jax.random.normal(splits[3], (D,), jnp.float32), 0.099609375, 1.8984375).astype(jnp.bfloat16)
    w_query = gaussian(splits[4], (D, D), D ** -0.5, 0.125, ((0, 32),))
    w_key = gaussian(splits[5], (D, D), D ** -0.5, 0.125, ((0, 32),))
    w_value = gaussian(splits[6], (D, D), D ** -0.5, 0.125, ((0, 32),))
    w_out = gaussian(splits[7], (D, D), (D // 128) ** -0.5, 1.5, ((0, 32),))
    gain_query = jnp.clip(1.0 + 0.18 * jax.random.normal(splits[8], (D,), jnp.float32), 0.099609375, 1.8984375).astype(jnp.bfloat16)
    gain_key = jnp.clip(1.0 + 0.18 * jax.random.normal(splits[9], (D,), jnp.float32), 0.099609375, 1.8984375).astype(jnp.bfloat16)
    gain_ffn = jnp.clip(1.0 + 0.18 * jax.random.normal(splits[10], (D,), jnp.float32), 0.099609375, 1.8984375).astype(jnp.bfloat16)
    router = gaussian(splits[11], (D, E), D ** -0.5, 0.125, ((0, 32),))
    expert_gate = gaussian(splits[12], (E, D, FF), D ** -0.5, 0.125, ((0, 8), (1, 4)))
    expert_up = gaussian(splits[13], (E, D, FF), D ** -0.5, 0.125, ((0, 8), (1, 4)))
    expert_down = gaussian(splits[14], (E, FF, D), (max(FF // 64, 1)) ** -0.5, 1.5, ((0, 8), (1, 4)))
    clip_flags = place_ends(jax.random.randint(splits[15], (H,), 0, 2), jax.random.fold_in(splits[15], 1), 0, 1).astype(jnp.int32)
    clip_factors = jnp.clip(jnp.exp(jax.random.uniform(splits[16], (H,), jnp.float32, math.log(0.25), math.log(1.0))), 0.25, 1.0)
    return dict(tokens=tokens, cotangent=cotangent, route_ids=route_ids, gain_attn=gain_attn, w_query=w_query, w_key=w_key, w_value=w_value, w_out=w_out, gain_query=gain_query, gain_key=gain_key, gain_ffn=gain_ffn, router=router, expert_gate=expert_gate, expert_up=expert_up, expert_down=expert_down, clip_flags=clip_flags, clip_factors=clip_factors)


EPSILON = 1e-05
PRECISE = lax.Precision.HIGHEST

@jax.custom_vjp
def low(v):
    return lax.optimization_barrier(v.astype(jnp.bfloat16)).astype(jnp.float32)

@jax.custom_vjp
def low_back(v):
    return v

def low_keep(v):
    return (low(v), None)

def low_pass(kept, grad):
    return (grad,)

def back_keep(v):
    return (v, None)

def back_low(kept, grad):
    return (low(grad),)
low.defvjp(low_keep, low_pass)
low_back.defvjp(back_keep, back_low)

def matmul(left, right):
    return jnp.dot(left, right, preferred_element_type=jnp.float32, precision=PRECISE)

def rms_norm(values, gain):
    factor = lax.rsqrt(lax.optimization_barrier(jnp.mean(values * values, axis=-1, keepdims=True)) + EPSILON)
    return values * factor * gain

def positions():
    row_index = jnp.arange(GROUP_TOK, dtype=jnp.int32)
    return jnp.where(row_index < PROMPT, row_index, PROMPT + (row_index - PROMPT) % CONT_LEN)

def rotary(values, position):
    inverse_freq = 10000.0 ** (-(jnp.arange(HD // 2, dtype=jnp.float32) * 2.0) / HD)
    phase_angle = position.astype(jnp.float32)[:, None] * inverse_freq[None, :]
    cosine_table = jnp.concatenate([jnp.cos(phase_angle), jnp.cos(phase_angle)], axis=-1)[:, None, :]
    sine_table = jnp.concatenate([jnp.sin(phase_angle), jnp.sin(phase_angle)], axis=-1)[:, None, :]
    shaped = values.reshape(values.shape[:-1] + (H, HD))
    front_half = shaped[..., :HD // 2]
    back_half = shaped[..., HD // 2:]
    turned = jnp.concatenate([-back_half, front_half], axis=-1)
    return (shaped * cosine_table + turned * sine_table).reshape(values.shape)

def visible_pairs():
    query_rows = jnp.arange(GROUP_TOK, dtype=jnp.int32)[:, None]
    key_rows = jnp.arange(GROUP_TOK, dtype=jnp.int32)[None, :]
    same_cont = (key_rows - PROMPT) // CONT_LEN == (query_rows - PROMPT) // CONT_LEN
    return (key_rows <= query_rows) & ((key_rows < PROMPT) | same_cont)

def group_attention(visible, pieces):
    query_rows, key_rows, value_rows = pieces
    shape4 = (GROUP_TOK, H, HD)
    raw_scores = jnp.einsum('rhe,khe->hrk', query_rows.reshape(shape4), key_rows.reshape(shape4), precision=PRECISE)
    scores = low_back(raw_scores * HD ** (-0.5))
    masked = jnp.where(visible[None], scores, -1e+30)
    head_peak = lax.optimization_barrier(jnp.max(masked, axis=(1, 2)))
    weights = low(jax.nn.softmax(masked, axis=-1))
    mixed = jnp.einsum('hrk,khe->rhe', weights, value_rows.reshape(shape4), precision=PRECISE)
    return (mixed.reshape(GROUP_TOK, D), head_peak)

def route_slots(route_ids):
    block_count = GROUPS * N_SEQ
    blocks = route_ids.reshape(block_count, ROWS * TOP).astype(jnp.int32)
    onehot = (blocks[:, :, None] == jnp.arange(E, dtype=jnp.int32)[None, None, :]).astype(jnp.int32)
    before = jnp.cumsum(onehot, axis=1, dtype=jnp.int32) - onehot
    slot_place = lax.optimization_barrier(jnp.sum(before * onehot, axis=2, dtype=jnp.int32))
    block_ids = jnp.arange(block_count, dtype=jnp.int32)[:, None]
    slot_index = ((blocks * block_count + block_ids) * CAP_G + slot_place).astype(jnp.int32)
    route_index = jnp.arange(block_count * ROWS * TOP, dtype=jnp.int32)
    slot_table = jnp.zeros((E * block_count * CAP_G,), jnp.int32).at[slot_index.reshape(-1)].set(route_index + 1)
    return slot_table.reshape(E, block_count * CAP_G)

def expert_part(hidden_mid, gate_prob, source, gate_w, up_w, down_w, expert):
    filled = source > 0
    route_index = jnp.where(filled, source - 1, 0)
    token_index = route_index // TOP
    rows_in = low_back(hidden_mid[token_index] * filled[:, None].astype(jnp.float32))
    gate_val = low_back(matmul(rows_in, gate_w))
    up_val = low_back(matmul(rows_in, up_w))
    hidden = low(jax.nn.silu(gate_val) * up_val)
    expert_out = low(low_back(matmul(hidden, down_w)))
    weight = gate_prob[token_index, expert] * filled.astype(jnp.float32)
    return weight[:, None] * expert_out

def reference(tokens, cotangent, route_ids, gain_attn, w_query, w_key, w_value, w_out, gain_query, gain_key, gain_ffn, router, expert_gate, expert_up, expert_down, clip_flags, clip_factors):
    head_scale = jnp.where(clip_flags == 1, jnp.sqrt(clip_factors), jnp.ones_like(clip_factors))
    column_scale = jnp.repeat(head_scale, HD)
    clipped_query = (w_query.astype(jnp.float32) * column_scale[None, :]).astype(jnp.bfloat16)
    clipped_key = (w_key.astype(jnp.float32) * column_scale[None, :]).astype(jnp.bfloat16)
    slot_table = route_slots(route_ids)
    position = positions()
    visible = visible_pairs()
    grouped = (GROUPS, GROUP_TOK, D)

    def forward(inputs, attn_gain, query_w, key_w, value_w, out_w, query_gain, key_gain, ffn_gain, router_w, gate_w, up_w, down_w):
        flat_in = inputs.reshape(GROUPS * GROUP_TOK, D)
        hidden_in = low(rms_norm(flat_in, attn_gain))
        query_raw = low_back(matmul(hidden_in, low(query_w * column_scale[None, :])))
        key_raw = low_back(matmul(hidden_in, low(key_w * column_scale[None, :])))
        value_all = low(low_back(matmul(hidden_in, value_w)))
        query_all = low(rotary(rms_norm(query_raw, query_gain).reshape(grouped), position))
        key_all = low(rotary(rms_norm(key_raw, key_gain).reshape(grouped), position))
        mixed, peaks = lax.map(jax.checkpoint(partial(group_attention, visible)), (query_all, key_all, value_all.reshape(grouped)))
        attended = low(low_back(mixed.reshape(GROUPS * GROUP_TOK, D)))
        residual_mid = flat_in + low_back(matmul(attended, out_w))
        hidden_mid = low(rms_norm(residual_mid, ffn_gain))
        gate_prob = jax.nn.softmax(matmul(hidden_mid, router_w), axis=-1)

        def step(running, pieces):
            source, gate_e, up_e, down_e, expert = pieces
            part = jax.checkpoint(expert_part)(hidden_mid, gate_prob, source, gate_e, up_e, down_e, expert)
            token_index = jnp.where(source > 0, source - 1, 0) // TOP
            return (running.at[token_index].add(part), None)
        start = jnp.zeros((GROUPS * GROUP_TOK, D), jnp.float32)
        ffn_out, unused = lax.scan(step, start, (slot_table, gate_w, up_w, down_w, jnp.arange(E, dtype=jnp.int32)))
        return ((residual_mid + ffn_out).reshape(grouped), lax.optimization_barrier(jnp.max(peaks, axis=0)))
    floats = [array.astype(jnp.float32) for array in (tokens, gain_attn, w_query, w_key, w_value, w_out, gain_query, gain_key, gain_ffn, router, expert_gate, expert_up, expert_down)]
    block, pullback, max_logit = jax.vjp(forward, *floats, has_aux=True)
    grads = pullback(cotangent.astype(jnp.float32))
    return (block.astype(jnp.bfloat16), grads[0], grads[1], grads[2], grads[3], grads[4], grads[5], grads[6], grads[7], grads[8], grads[9], grads[10], grads[11], grads[12], max_logit, clipped_query, clipped_key)
```

```python
import functools

import jax
import jax.numpy as jnp
from jax import lax
from jax.experimental import pallas as pl
from jax.experimental.pallas import tpu as pltpu
from jax.sharding import PartitionSpec as P

D = 2048
H = 16
HD = 128
TOP = 8
E = 16
PROMPT = 1024
CONT_LEN = 128

EPSILON = 1e-05
SCALE = HD ** (-0.5)
NEG = -1e30
BLOCK = 256
F32 = jnp.float32
BF16 = jnp.bfloat16


def dot(left, right, dims):
    return lax.dot_general(left, right, (dims, ((), ())), preferred_element_type=F32)


def mm(left, right):
    return dot(left, right, ((1,), (0,)))


def mm_nt(left, right):
    return dot(left, right, ((1,), (1,)))


def mm_tn(left, right):
    return dot(left, right, ((0,), (0,)))


def batched(left, right, left_dim, right_dim):
    return lax.dot_general(
        left, right, (((left_dim,), (right_dim,)), ((0,), (0,))), preferred_element_type=F32
    )


def normalize(values):
    factor = lax.rsqrt(jnp.mean(values * values, axis=-1, keepdims=True) + EPSILON)
    return (values * factor, factor)


def norm_back(grad_normed, normed, factor):
    return factor * (grad_normed - normed * jnp.mean(grad_normed * normed, axis=-1, keepdims=True))


def rotary_tables(total):
    row = jnp.arange(total, dtype=jnp.int32)
    position = jnp.where(row < PROMPT, row, PROMPT + (row - PROMPT) % CONT_LEN)
    inverse_freq = 10000.0 ** (-(jnp.arange(HD // 2, dtype=F32) * 2.0) / HD)
    phase = position.astype(F32)[:, None] * inverse_freq[None, :]
    cosine, sine = jnp.cos(phase), jnp.sin(phase)
    return (
        jnp.concatenate([cosine, cosine], axis=-1),
        jnp.concatenate([-sine, sine], axis=-1),
    )


def prep_kernel(q_in, k_in, v_in, sums, gain_q, gain_k, cos_ref, sin_ref, q_out, k_out, v_out):
    factors = lax.rsqrt(sums[...] * (1.0 / D) + EPSILON)
    cosine, sine = cos_ref[...], sin_ref[...]
    for source, gain, out, col in ((q_in, gain_q, q_out, 0), (k_in, gain_k, k_out, 1)):
        factor = factors[:, col : col + 1]
        for head in range(source.shape[1] // HD):
            cut = slice(head * HD, (head + 1) * HD)
            values = source[:, cut] * factor * gain[:, cut]
            out[:, cut] = (values * cosine + pltpu.roll(values, HD // 2, 1) * sine).astype(BF16)
    v_out[...] = v_in[...].astype(BF16)


def prep(qkv, sums, gain_q, gain_k, cosine, sine):
    total, width = qkv.shape
    cols = width // 3
    rows = pl.BlockSpec((BLOCK, HD), lambda i: (i, 0))

    def part(at):
        return pl.BlockSpec((BLOCK, cols), lambda i: (i, at))

    whole = pl.BlockSpec((1, cols), lambda i: (0, 0))
    return pl.pallas_call(
        prep_kernel,
        grid=(total // BLOCK,),
        in_specs=[
            part(0),
            part(1),
            part(2),
            pl.BlockSpec((BLOCK, 2), lambda i: (i, 0)),
            whole,
            whole,
            rows,
            rows,
        ],
        out_specs=[part(0)] * 3,
        out_shape=[jax.ShapeDtypeStruct((total, cols), BF16)] * 3,
        cost_estimate=pl.CostEstimate(
            flops=8 * total * cols, bytes_accessed=18 * total * cols, transcendentals=0
        ),
        name="qk_prep",
    )(qkv, qkv, qkv, sums, gain_q, gain_k, cosine, sine)


def block_scores(index, query, k_ref):
    keys = k_ref[pl.ds(pl.multiple_of(index * BLOCK, BLOCK), BLOCK), :]
    first = mm_nt(query, k_ref[:PROMPT, :]) * SCALE
    row = index * BLOCK + lax.broadcasted_iota(jnp.int32, first.shape, 0)
    col = lax.broadcasted_iota(jnp.int32, first.shape, 1)
    first = jnp.where(col <= row, first, NEG)
    own = mm_nt(query, keys) * SCALE
    row = lax.broadcasted_iota(jnp.int32, own.shape, 0)
    col = lax.broadcasted_iota(jnp.int32, own.shape, 1)
    seen = (row // CONT_LEN == col // CONT_LEN) & (col <= row) & (index * BLOCK + row >= PROMPT)
    own = jnp.where(seen, own, NEG)
    peak = jnp.maximum(
        jnp.max(first, axis=-1, keepdims=True), jnp.max(own, axis=-1, keepdims=True)
    )
    first = jnp.exp(first - peak)
    own = jnp.exp(own - peak)
    total = jnp.sum(first, axis=-1, keepdims=True) + jnp.sum(own, axis=-1, keepdims=True)
    inverse = 1.0 / total
    return (first * inverse, own * inverse, peak, keys)


def attn_kernel(q_ref, k_ref, v_ref, out_ref, peak_ref):
    index = pl.program_id(1)
    first, own, peak, _ = block_scores(index, q_ref[...], k_ref)
    values = v_ref[pl.ds(pl.multiple_of(index * BLOCK, BLOCK), BLOCK), :]
    mixed = mm(first.astype(BF16), v_ref[:PROMPT, :]) + mm(own.astype(BF16), values)
    out_ref[...] = mixed.astype(BF16)
    highest = jnp.broadcast_to(jnp.max(peak, axis=0, keepdims=True), peak_ref.shape)

    @pl.when(index == 0)
    def _():
        peak_ref[...] = highest

    @pl.when(index > 0)
    def _():
        peak_ref[...] = jnp.maximum(peak_ref[...], highest)


def attn_cost(total, heads, dots):
    pairs = total * (PROMPT + BLOCK) * heads
    return pl.CostEstimate(
        flops=2 * HD * dots * pairs, bytes_accessed=8 * total * heads * HD, transcendentals=pairs
    )


def attention(query, key, value):
    total, cols = query.shape
    heads = cols // HD
    full = pl.BlockSpec((total, HD), lambda h, i: (0, h))
    block = pl.BlockSpec((BLOCK, HD), lambda h, i: (i, h))
    return pl.pallas_call(
        attn_kernel,
        grid=(heads, total // BLOCK),
        in_specs=[block, full, full],
        out_specs=[block, pl.BlockSpec((None, 8, HD), lambda h, i: (h, 0, 0))],
        out_shape=[
            jax.ShapeDtypeStruct((total, cols), BF16),
            jax.ShapeDtypeStruct((heads, 8, HD), F32),
        ],
        cost_estimate=attn_cost(total, heads, 2),
        name="attn_fwd",
    )(query, key, value)


def rotate_back(values, cosine, sine):
    return values * cosine - pltpu.roll(values, HD // 2, 1) * sine


def attn_back_kernel(
    q_ref, k_ref, v_ref, do_ref, cosb_ref, sinb_ref, cos_ref, sin_ref, dq_ref, dk_ref, dv_ref, dk_acc, dv_acc
):
    index = pl.program_id(1)
    here = pl.ds(pl.multiple_of(index * BLOCK, BLOCK), BLOCK)

    @pl.when(index == 0)
    def _():
        dk_acc[...] = jnp.zeros_like(dk_acc)
        dv_acc[...] = jnp.zeros_like(dv_acc)

    query, grad = q_ref[...], do_ref[...]
    first, own, _, keys = block_scores(index, query, k_ref)
    grad_first = mm_nt(grad, v_ref[:PROMPT, :])
    grad_own = mm_nt(grad, v_ref[here, :])
    delta = jnp.sum(first * grad_first, axis=-1, keepdims=True) + jnp.sum(
        own * grad_own, axis=-1, keepdims=True
    )
    grad_first = (first * (grad_first - delta)).astype(BF16)
    grad_own = (own * (grad_own - delta)).astype(BF16)
    first, own = first.astype(BF16), own.astype(BF16)
    dv_acc[:PROMPT, :] += mm_tn(first, grad)
    dv_acc[here, :] += mm_tn(own, grad)
    dk_acc[:PROMPT, :] += mm_tn(grad_first, query)
    dk_acc[here, :] += mm_tn(grad_own, query)
    dq = (mm(grad_first, k_ref[:PROMPT, :]) + mm(grad_own, keys)) * SCALE
    dq_ref[...] = rotate_back(dq, cosb_ref[...], sinb_ref[...])

    @pl.when(index == pl.num_programs(1) - 1)
    def _():
        dk_ref[...] = rotate_back(dk_acc[...] * SCALE, cos_ref[...], sin_ref[...])
        dv_ref[...] = dv_acc[...].astype(BF16)


def attention_back(query, key, value, grad, cosine, sine):
    total, cols = query.shape
    heads = cols // HD
    full = pl.BlockSpec((total, HD), lambda h, i: (0, h))
    block = pl.BlockSpec((BLOCK, HD), lambda h, i: (i, h))
    table = pl.BlockSpec((BLOCK, HD), lambda h, i: (i, 0))
    table_full = pl.BlockSpec((total, HD), lambda h, i: (0, 0))
    return pl.pallas_call(
        attn_back_kernel,
        grid=(heads, total // BLOCK),
        in_specs=[block, full, full, block, table, table, table_full, table_full],
        out_specs=[block, full, full],
        out_shape=[
            jax.ShapeDtypeStruct((total, cols), F32),
            jax.ShapeDtypeStruct((total, cols), F32),
            jax.ShapeDtypeStruct((total, cols), BF16),
        ],
        scratch_shapes=[pltpu.VMEM((total, HD), F32), pltpu.VMEM((total, HD), F32)],
        cost_estimate=attn_cost(total, heads, 5),
        name="attn_back",
    )(query, key, value, grad, cosine, sine, cosine, sine)


def per_device(
    n_grp,
    n_seq,
    tokens,
    cotangent,
    route_ids,
    gain_attn,
    w_query,
    w_key,
    w_value,
    w_out,
    gain_query,
    gain_key,
    gain_ffn,
    router,
    expert_gate,
    expert_up,
    expert_down,
    clip_flags,
    clip_factors,
):
    n_all = n_grp * n_seq
    both = ("grp", "seq")
    rows = tokens.shape[1]
    total = rows * n_seq
    share = D // n_all
    cols = D // n_seq
    heads = H // n_seq
    local_e = E // n_seq
    capacity = 9 * rows * TOP // (8 * E)
    seq = lax.axis_index("seq")
    tokens, cotangent, route_ids = tokens[0], cotangent[0], route_ids[0]

    head_scale = jnp.where(clip_flags == 1, jnp.sqrt(clip_factors), jnp.ones_like(clip_factors))
    column_scale = jnp.broadcast_to(head_scale[:, None], (H, HD)).reshape(D)
    clipped_query = (w_query.astype(F32) * column_scale[None, :]).astype(BF16)
    clipped_key = (w_key.astype(F32) * column_scale[None, :]).astype(BF16)

    tokens_all = lax.all_gather(tokens, "seq", axis=0, tiled=True)

    small = jnp.concatenate(
        [gain_attn[None], gain_query[None], gain_key[None], gain_ffn[None], router.T], axis=0
    ).reshape(1, (4 + E) * share)
    small = lax.all_gather(small, both, axis=0, tiled=True)
    small = small.reshape(n_all, 4 + E, share).transpose(1, 0, 2).reshape(4 + E, D)
    gains = small[:4].astype(F32)
    attn_gain, query_gain, key_gain, ffn_gain = gains[0:1], gains[1:2], gains[2:3], gains[3:4]
    router_t = small[4:]
    query_gain = lax.dynamic_slice(query_gain, (0, seq * cols), (1, cols))
    key_gain = lax.dynamic_slice(key_gain, (0, seq * cols), (1, cols))

    w_qkv = jnp.stack([clipped_query, clipped_key, w_value], axis=1)
    w_qkv = w_qkv.reshape(share, 3, n_seq, cols).transpose(2, 0, 1, 3)
    w_qkv = w_qkv.reshape(n_seq, share, 3 * cols)
    w_qkv = lax.all_to_all(w_qkv, "seq", split_axis=0, concat_axis=0, tiled=True)
    w_qkv = lax.all_gather(w_qkv.reshape(n_seq * share, 3 * cols), "grp", axis=0, tiled=True)

    cosine, sine = rotary_tables(total)

    route_all = lax.all_gather(route_ids, "seq", axis=0, tiled=True).reshape(n_seq, rows, TOP)
    row_at = lax.broadcasted_iota(jnp.int32, (rows, rows), 0)
    col_at = lax.broadcasted_iota(jnp.int32, (rows, rows), 1)
    earlier = (row_at < col_at).astype(BF16)
    slot_at = lax.broadcasted_iota(jnp.int32, (n_seq, capacity, rows), 1)
    picks = []
    for e in range(local_e):
        hit = jnp.any(route_all == seq * local_e + e, axis=-1)
        place = mm(hit.astype(BF16), earlier).astype(jnp.int32)
        picks.append(hit[:, None, :] & (place[:, None, :] == slot_at))

    inputs_all = tokens_all.astype(F32)
    hidden_in = (normalize(inputs_all)[0] * attn_gain).astype(BF16)
    qkv = mm(hidden_in, w_qkv)
    raw_q, raw_k = qkv[:, :cols], qkv[:, cols : 2 * cols]
    sums = jnp.stack([jnp.sum(raw_q * raw_q, axis=-1), jnp.sum(raw_k * raw_k, axis=-1)], axis=0)
    sums = lax.psum(sums, "seq")
    query, key, value = prep(qkv, sums.T, query_gain, key_gain, cosine, sine)
    attended_cols, peaks = attention(query, key, value)
    max_logit = lax.all_gather(peaks[:, 0, 0], "seq", axis=0, tiled=True)
    max_logit = lax.pmax(max_logit, "grp")

    attended = lax.all_to_all(attended_cols, "seq", split_axis=0, concat_axis=1, tiled=True)
    w_out_all = lax.all_gather(w_out, both, axis=0, tiled=True)
    inputs = tokens.astype(F32)
    residual_mid = inputs + mm(attended, w_out_all)
    normed_mid, factor_mid = normalize(residual_mid)
    hidden_mid = (normed_mid * ffn_gain).astype(BF16)
    hidden_all = lax.all_gather(hidden_mid, "seq", axis=0, tiled=True)
    gate_prob = jax.nn.softmax(mm_nt(hidden_mid, router_t), axis=-1)
    gate_prob_all = jax.nn.softmax(mm_nt(hidden_all, router_t), axis=-1)

    gate_w = lax.all_gather(expert_gate, "grp", axis=1, tiled=True)
    up_w = lax.all_gather(expert_up, "grp", axis=1, tiled=True)
    down_w = lax.all_gather(expert_down, "grp", axis=1, tiled=True)
    cotangent_all = lax.all_gather(cotangent, "seq", axis=0, tiled=True)

    hidden_blocks = hidden_all.reshape(n_seq, rows, D)
    cotangent_blocks = cotangent_all.reshape(n_seq, rows, D)
    expert_at = lax.broadcasted_iota(jnp.int32, gate_prob_all.shape, 1)
    mixed_out = jnp.zeros((n_seq, rows, D), F32)
    mixed_grad = jnp.zeros((n_seq, rows, D), F32)
    weight_rows, gate_grads, up_grads, down_grads = [], [], [], []
    for e in range(local_e):
        pick = picks[e].astype(BF16)
        prob = jnp.sum(jnp.where(expert_at == seq * local_e + e, gate_prob_all, 0.0), axis=-1)
        prob = prob.reshape(n_seq, 1, rows)
        weighted = jnp.where(picks[e], prob, 0.0)
        slot_weight = jnp.sum(weighted, axis=-1).reshape(n_seq * capacity, 1)
        received = batched(pick, hidden_blocks, 2, 1).astype(BF16).reshape(n_seq * capacity, D)
        gate_val = mm(received, gate_w[e])
        up_val = mm(received, up_w[e])
        sigmoid_gate = jax.nn.sigmoid(gate_val)
        silu_gate = gate_val * sigmoid_gate
        hidden = (silu_gate * up_val).astype(BF16)
        expert_out = mm(hidden, down_w[e]).astype(BF16)
        out_blocks = expert_out.reshape(n_seq, capacity, D)
        mixed_out = mixed_out + batched(weighted.astype(BF16), out_blocks, 1, 1)

        grad_slot = batched(pick, cotangent_blocks, 2, 1).reshape(n_seq * capacity, D)
        slot_dot = jnp.sum(grad_slot * expert_out.astype(F32), axis=-1)
        slot_dot = slot_dot.reshape(n_seq, capacity, 1)
        weight_rows.append(jnp.sum(jnp.where(picks[e], slot_dot, 0.0), axis=1))
        grad_received = (slot_weight * grad_slot).astype(BF16)
        grad_hidden = mm_nt(grad_received, down_w[e])
        grad_gate = (
            grad_hidden * up_val * sigmoid_gate * (1.0 + gate_val * (1.0 - sigmoid_gate))
        ).astype(BF16)
        grad_up = (grad_hidden * silu_gate).astype(BF16)
        grad_rows = (mm_nt(grad_gate, gate_w[e]) + mm_nt(grad_up, up_w[e])).astype(BF16)
        mixed_grad = mixed_grad + batched(pick, grad_rows.reshape(n_seq, capacity, D), 1, 1)
        down_grads.append(mm_tn(hidden, grad_received).astype(BF16))
        gate_grads.append(mm_tn(received, grad_gate).astype(BF16))
        up_grads.append(mm_tn(received, grad_up).astype(BF16))

    mixed_grad = mixed_grad.reshape(total, D).astype(BF16)
    grad_hidden_mid = lax.psum_scatter(mixed_grad, "seq", scatter_dimension=0, tiled=True)
    mixed_out = mixed_out.reshape(total, D).astype(BF16)
    ffn_out = lax.psum_scatter(mixed_out, "seq", scatter_dimension=0, tiled=True)
    block_out = (residual_mid + ffn_out.astype(F32)).astype(BF16)

    weight_rows = jnp.stack(weight_rows, axis=1)
    weight_rows = lax.all_to_all(weight_rows, "seq", split_axis=0, concat_axis=0, tiled=True)
    grad_prob = weight_rows.reshape(E, rows).T
    grad_logits = gate_prob * (grad_prob - jnp.sum(gate_prob * grad_prob, axis=-1, keepdims=True))
    grad_router = mm_tn(grad_logits, hidden_mid.astype(F32))
    grad_hidden_mid = grad_hidden_mid.astype(F32) + mm(grad_logits, router_t.astype(F32))
    grad_ffn_gain = jnp.sum(grad_hidden_mid * normed_mid, axis=0)
    grad_mid = cotangent.astype(F32) + norm_back(grad_hidden_mid * ffn_gain, normed_mid, factor_mid)
    grad_attn = grad_mid.astype(BF16)
    grad_attended = mm_nt(grad_attn, w_out_all).astype(BF16)
    grad_attended = lax.all_to_all(grad_attended, "seq", split_axis=1, concat_axis=0, tiled=True)

    grad_q, grad_k, grad_v = attention_back(query, key, value, grad_attended, cosine, sine)
    factor_q = lax.rsqrt(sums[0] * (1.0 / D) + EPSILON)[:, None]
    factor_k = lax.rsqrt(sums[1] * (1.0 / D) + EPSILON)[:, None]
    normed_q, normed_k = raw_q * factor_q, raw_k * factor_k
    prod_q, prod_k = grad_q * normed_q, grad_k * normed_k
    grad_query_gain = jnp.sum(prod_q, axis=0)
    grad_key_gain = jnp.sum(prod_k, axis=0)
    means = jnp.stack(
        [jnp.sum(prod_q * query_gain, axis=-1), jnp.sum(prod_k * key_gain, axis=-1)], axis=0
    )
    means = lax.psum(means, "seq") * (1.0 / D)
    grad_q = factor_q * (grad_q * query_gain - normed_q * means[0][:, None])
    grad_k = factor_k * (grad_k * key_gain - normed_k * means[1][:, None])
    grad_qkv = jnp.concatenate([grad_q.astype(BF16), grad_k.astype(BF16), grad_v], axis=1)

    grad_hidden_in = mm_nt(grad_qkv, w_qkv).astype(BF16)
    grad_hidden_in = lax.psum_scatter(grad_hidden_in, "seq", scatter_dimension=0, tiled=True)
    grad_hidden_in = grad_hidden_in.astype(F32)

    grad_w = mm_tn(hidden_in, grad_qkv).astype(BF16)
    grad_w = lax.psum_scatter(grad_w, "grp", scatter_dimension=0, tiled=True)
    grad_w = grad_w.reshape(n_seq, share, 3 * cols)
    grad_w = lax.all_to_all(grad_w, "seq", split_axis=0, concat_axis=0, tiled=True)
    grad_w = grad_w.astype(F32).reshape(n_seq, share, 3, cols).transpose(2, 1, 0, 3)
    grad_w = grad_w.reshape(3, share, D)
    grad_query_w = grad_w[0] * column_scale[None, :]
    grad_key_w = grad_w[1] * column_scale[None, :]
    grad_value_w = grad_w[2]

    grad_attn_all = lax.all_gather(grad_attn, "seq", axis=0, tiled=True)
    attended_own = attended.reshape(rows, n_grp, n_seq, share).transpose(2, 0, 1, 3)
    attended_own = attended_own.reshape(n_seq * rows, n_grp * share)
    attended_own = lax.all_to_all(attended_own, "seq", split_axis=0, concat_axis=0, tiled=True)
    grad_out_w = mm_tn(attended_own, grad_attn_all).astype(BF16)
    grad_out_w = lax.psum_scatter(grad_out_w, "grp", scatter_dimension=0, tiled=True).astype(F32)

    normed_in, factor_in = normalize(inputs)
    grad_attn_gain = jnp.sum(grad_hidden_in * normed_in, axis=0)
    tokens_grad = grad_mid + norm_back(grad_hidden_in * attn_gain, normed_in, factor_in)

    def spread(part):
        return lax.dynamic_update_slice(jnp.zeros((D,), F32), part, (seq * cols,))

    late = jnp.concatenate(
        [
            grad_router,
            grad_ffn_gain[None],
            grad_attn_gain[None],
            spread(grad_query_gain)[None],
            spread(grad_key_gain)[None],
        ],
        axis=0,
    )
    late = late.reshape(E + 4, n_all, share).transpose(1, 0, 2).reshape(n_all, (E + 4) * share)
    late = lax.psum_scatter(late, both, scatter_dimension=0, tiled=True).reshape(E + 4, share)

    def expert_share(parts):
        summed = lax.psum_scatter(jnp.stack(parts), "grp", scatter_dimension=1, tiled=True)
        return summed.astype(F32)

    return (
        block_out[None],
        tokens_grad[None],
        late[E + 1],
        grad_query_w,
        grad_key_w,
        grad_value_w,
        grad_out_w,
        late[E + 2],
        late[E + 3],
        late[E],
        late[:E].T,
        expert_share(gate_grads),
        expert_share(up_grads),
        expert_share(down_grads),
        max_logit,
        clipped_query,
        clipped_key,
    )


def solution(mesh):
    rows = P("grp", "seq", None)
    vector = P(("grp", "seq"))
    matrix = P(("grp", "seq"), None)
    expert = P("seq", "grp", None)
    return jax.shard_map(
        functools.partial(per_device, mesh.shape["grp"], mesh.shape["seq"]),
        mesh=mesh,
        in_specs=(rows, rows, rows, vector)
        + (matrix,) * 4
        + (vector,) * 3
        + (matrix,)
        + (expert,) * 3
        + (P(), P()),
        out_specs=(rows, rows, vector)
        + (matrix,) * 4
        + (vector,) * 3
        + (matrix,)
        + (expert,) * 3
        + (P(), matrix, matrix),
        check_vma=False,
    )
```

```python
import functools

import jax
import jax.numpy as jnp
from jax import lax
from jax.experimental import pallas as pl
from jax.experimental.pallas import tpu as pltpu
from jax.sharding import PartitionSpec as P

D = 2048
H = 16
HD = 128
TOP = 8
E = 16
PROMPT = 1024
CONT_LEN = 128

EPSILON = 1e-05
SCALE = HD ** (-0.5)
NEG = -1e30
BLOCK = 256
F32 = jnp.float32
BF16 = jnp.bfloat16


def dot(left, right, dims):
    return lax.dot_general(left, right, (dims, ((), ())), preferred_element_type=F32)


def mm(left, right):
    return dot(left, right, ((1,), (0,)))


def mm_nt(left, right):
    return dot(left, right, ((1,), (1,)))


def mm_tn(left, right):
    return dot(left, right, ((0,), (0,)))


def batched(left, right, left_dim, right_dim):
    return lax.dot_general(
        left, right, (((left_dim,), (right_dim,)), ((0,), (0,))), preferred_element_type=F32
    )


def normalize(values):
    factor = lax.rsqrt(jnp.mean(values * values, axis=-1, keepdims=True) + EPSILON)
    return (values * factor, factor)


def norm_back(grad_normed, normed, factor):
    return factor * (grad_normed - normed * jnp.mean(grad_normed * normed, axis=-1, keepdims=True))


def rotary_tables(total):
    row = jnp.arange(total, dtype=jnp.int32)
    position = jnp.where(row < PROMPT, row, PROMPT + (row - PROMPT) % CONT_LEN)
    inverse_freq = 10000.0 ** (-(jnp.arange(HD // 2, dtype=F32) * 2.0) / HD)
    phase = position.astype(F32)[:, None] * inverse_freq[None, :]
    cosine, sine = jnp.cos(phase), jnp.sin(phase)
    return (
        jnp.concatenate([cosine, cosine], axis=-1),
        jnp.concatenate([-sine, sine], axis=-1),
    )


def prep_kernel(q_in, k_in, v_in, sums, gain_q, gain_k, cos_ref, sin_ref, q_out, k_out, v_out):
    factors = lax.rsqrt(sums[...] * (1.0 / D) + EPSILON)
    cosine, sine = cos_ref[...], sin_ref[...]
    for source, gain, out, col in ((q_in, gain_q, q_out, 0), (k_in, gain_k, k_out, 1)):
        factor = factors[:, col : col + 1]
        for head in range(source.shape[1] // HD):
            cut = slice(head * HD, (head + 1) * HD)
            values = source[:, cut] * factor * gain[:, cut]
            out[:, cut] = (values * cosine + pltpu.roll(values, HD // 2, 1) * sine).astype(BF16)
    v_out[...] = v_in[...].astype(BF16)


def prep(qkv, sums, gain_q, gain_k, cosine, sine):
    total, width = qkv.shape
    cols = width // 3
    rows = pl.BlockSpec((BLOCK, HD), lambda i: (i, 0))

    def part(at):
        return pl.BlockSpec((BLOCK, cols), lambda i: (i, at))

    whole = pl.BlockSpec((1, cols), lambda i: (0, 0))
    return pl.pallas_call(
        prep_kernel,
        grid=(total // BLOCK,),
        in_specs=[
            part(0),
            part(1),
            part(2),
            pl.BlockSpec((BLOCK, 2), lambda i: (i, 0)),
            whole,
            whole,
            rows,
            rows,
        ],
        out_specs=[part(0)] * 3,
        out_shape=[jax.ShapeDtypeStruct((total, cols), BF16)] * 3,
        cost_estimate=pl.CostEstimate(
            flops=8 * total * cols, bytes_accessed=18 * total * cols, transcendentals=0
        ),
        name="qk_prep",
    )(qkv, qkv, qkv, sums, gain_q, gain_k, cosine, sine)


def block_scores(index, query, k_ref):
    keys = k_ref[pl.ds(pl.multiple_of(index * BLOCK, BLOCK), BLOCK), :]
    first = mm_nt(query, k_ref[:PROMPT, :]) * SCALE
    row = index * BLOCK + lax.broadcasted_iota(jnp.int32, first.shape, 0)
    col = lax.broadcasted_iota(jnp.int32, first.shape, 1)
    first = jnp.where(col <= row, first, NEG)
    own = mm_nt(query, keys) * SCALE
    row = lax.broadcasted_iota(jnp.int32, own.shape, 0)
    col = lax.broadcasted_iota(jnp.int32, own.shape, 1)
    seen = (row // CONT_LEN == col // CONT_LEN) & (col <= row) & (index * BLOCK + row >= PROMPT)
    own = jnp.where(seen, own, NEG)
    peak = jnp.maximum(
        jnp.max(first, axis=-1, keepdims=True), jnp.max(own, axis=-1, keepdims=True)
    )
    first = jnp.exp(first - peak)
    own = jnp.exp(own - peak)
    total = jnp.sum(first, axis=-1, keepdims=True) + jnp.sum(own, axis=-1, keepdims=True)
    inverse = 1.0 / total
    return (first * inverse, own * inverse, peak, keys)


def attn_kernel(q_ref, k_ref, v_ref, out_ref, peak_ref):
    index = pl.program_id(1)
    first, own, peak, _ = block_scores(index, q_ref[...], k_ref)
    values = v_ref[pl.ds(pl.multiple_of(index * BLOCK, BLOCK), BLOCK), :]
    mixed = mm(first.astype(BF16), v_ref[:PROMPT, :]) + mm(own.astype(BF16), values)
    out_ref[...] = mixed.astype(BF16)
    highest = jnp.broadcast_to(jnp.max(peak, axis=0, keepdims=True), peak_ref.shape)

    @pl.when(index == 0)
    def _():
        peak_ref[...] = highest

    @pl.when(index > 0)
    def _():
        peak_ref[...] = jnp.maximum(peak_ref[...], highest)


def attn_cost(total, heads, dots):
    pairs = total * (PROMPT + BLOCK) * heads
    return pl.CostEstimate(
        flops=2 * HD * dots * pairs, bytes_accessed=8 * total * heads * HD, transcendentals=pairs
    )


def attention(query, key, value):
    total, cols = query.shape
    heads = cols // HD
    full = pl.BlockSpec((total, HD), lambda h, i: (0, h))
    block = pl.BlockSpec((BLOCK, HD), lambda h, i: (i, h))
    return pl.pallas_call(
        attn_kernel,
        grid=(heads, total // BLOCK),
        in_specs=[block, full, full],
        out_specs=[block, pl.BlockSpec((None, 8, HD), lambda h, i: (h, 0, 0))],
        out_shape=[
            jax.ShapeDtypeStruct((total, cols), BF16),
            jax.ShapeDtypeStruct((heads, 8, HD), F32),
        ],
        cost_estimate=attn_cost(total, heads, 2),
        name="attn_fwd",
    )(query, key, value)


def rotate_back(values, cosine, sine):
    return values * cosine - pltpu.roll(values, HD // 2, 1) * sine


def attn_back_kernel(
    q_ref, k_ref, v_ref, do_ref, cosb_ref, sinb_ref, cos_ref, sin_ref, dq_ref, dk_ref, dv_ref, dk_acc, dv_acc
):
    index = pl.program_id(1)
    here = pl.ds(pl.multiple_of(index * BLOCK, BLOCK), BLOCK)

    @pl.when(index == 0)
    def _():
        dk_acc[...] = jnp.zeros_like(dk_acc)
        dv_acc[...] = jnp.zeros_like(dv_acc)

    query, grad = q_ref[...], do_ref[...]
    first, own, _, keys = block_scores(index, query, k_ref)
    grad_first = mm_nt(grad, v_ref[:PROMPT, :])
    grad_own = mm_nt(grad, v_ref[here, :])
    delta = jnp.sum(first * grad_first, axis=-1, keepdims=True) + jnp.sum(
        own * grad_own, axis=-1, keepdims=True
    )
    grad_first = (first * (grad_first - delta)).astype(BF16)
    grad_own = (own * (grad_own - delta)).astype(BF16)
    first, own = first.astype(BF16), own.astype(BF16)
    dv_acc[:PROMPT, :] += mm_tn(first, grad)
    dv_acc[here, :] += mm_tn(own, grad)
    dk_acc[:PROMPT, :] += mm_tn(grad_first, query)
    dk_acc[here, :] += mm_tn(grad_own, query)
    dq = (mm(grad_first, k_ref[:PROMPT, :]) + mm(grad_own, keys)) * SCALE
    dq_ref[...] = rotate_back(dq, cosb_ref[...], sinb_ref[...])

    @pl.when(index == pl.num_programs(1) - 1)
    def _():
        dk_ref[...] = rotate_back(dk_acc[...] * SCALE, cos_ref[...], sin_ref[...])
        dv_ref[...] = dv_acc[...].astype(BF16)


def attention_back(query, key, value, grad, cosine, sine):
    total, cols = query.shape
    heads = cols // HD
    full = pl.BlockSpec((total, HD), lambda h, i: (0, h))
    block = pl.BlockSpec((BLOCK, HD), lambda h, i: (i, h))
    table = pl.BlockSpec((BLOCK, HD), lambda h, i: (i, 0))
    table_full = pl.BlockSpec((total, HD), lambda h, i: (0, 0))
    return pl.pallas_call(
        attn_back_kernel,
        grid=(heads, total // BLOCK),
        in_specs=[block, full, full, block, table, table, table_full, table_full],
        out_specs=[block, full, full],
        out_shape=[
            jax.ShapeDtypeStruct((total, cols), F32),
            jax.ShapeDtypeStruct((total, cols), F32),
            jax.ShapeDtypeStruct((total, cols), BF16),
        ],
        scratch_shapes=[pltpu.VMEM((total, HD), F32), pltpu.VMEM((total, HD), F32)],
        cost_estimate=attn_cost(total, heads, 5),
        name="attn_back",
    )(query, key, value, grad, cosine, sine, cosine, sine)


def ring_order(n, width):
    depth = n // width
    order = [(z, 0) for z in range(depth)]
    for turn in range(depth):
        across = range(1, width) if turn % 2 == 0 else range(width - 1, 0, -1)
        order += [(depth - 1 - turn, x) for x in across]
    return [z * width + x for z, x in order]


class Ring:
    def __init__(self, n, width):
        self.n = n
        self.order = ring_order(n, width)
        place = [0] * n
        for at, index in enumerate(self.order):
            place[index] = at
        places = jnp.asarray(place, jnp.int32)
        self.place = places[lax.axis_index("seq")]
        self.owners = jnp.asarray(self.order, jnp.int32)[(self.place - jnp.arange(n)) % n]
        self.distance = (self.place - places) % n

    def shift(self, values, k):
        pairs = [(self.order[at], self.order[(at + k) % self.n]) for at in range(self.n)]
        return lax.ppermute(values, "seq", pairs)

    def gather(self, block):
        n, half = self.n, block.shape[0] // 2
        got = {0: (block[:half], block[half:])}
        for t in range(1, n // 2):
            got[t] = tuple(self.shift(part, 1) for part in got[t - 1])
            got[n - t] = tuple(self.shift(part, -1) for part in got[(n - t + 1) % n])
        got[n // 2] = (self.shift(got[n // 2 - 1][0], 1), self.shift(got[n // 2 + 1][1], -1))
        return [got[t] for t in range(n)]

    def scatter(self, part):
        n, mid = self.n, self.n // 2
        far = part(mid)
        down, up = [self.shift(far[0], -1), None], [None, self.shift(far[1], 1)]
        for t in range(mid - 1, 0, -1):
            near, other = part(t), part(n - t)
            down = [self.shift(join(near[i], down[i]), -1) for i in range(2)]
            up = [self.shift(join(other[i], up[i]), 1) for i in range(2)]
        own = part(0)
        return jnp.concatenate(
            [own[i].astype(F32) + down[i].astype(F32) + up[i].astype(F32) for i in range(2)], axis=0
        )

    def exchange(self, part):
        n = self.n
        return [part(0)] + [self.shift(part((n - t) % n), t) for t in range(1, n)]

    def ordered(self, pieces):
        return jnp.take(jnp.stack(pieces), self.distance, axis=0)


def join(values, running):
    return values if running is None else (values.astype(F32) + running.astype(F32)).astype(BF16)


class Group:
    def __init__(self, n):
        self.n = n
        self.chips = n // 2
        me = lax.axis_index("grp")
        self.chip, self.core = me // 2, me % 2

    def swap(self, values):
        return lax.ppermute(values, "grp", [(g, g ^ 1) for g in range(self.n)])

    def hop(self, values, k):
        pairs = [(g, (g + 2 * k) % self.n) for g in range(self.n)]
        return lax.ppermute(values, "grp", pairs)

    def gather(self, block):
        zeros = (0,) * block.ndim
        full = jnp.zeros((self.n,) + block.shape, block.dtype)
        for k in range(self.chips):
            here = block if k == 0 else self.hop(block, k)
            chip = (self.chip - k) % self.chips
            full = lax.dynamic_update_slice(full, here[None], (chip * 2 + self.core,) + zeros)
            other = self.swap(here)
            full = lax.dynamic_update_slice(full, other[None], (chip * 2 + 1 - self.core,) + zeros)
        return full

    def scatter(self, blocks):
        pairs = blocks.reshape((self.chips, 2) + blocks.shape[1:])
        mine = lax.dynamic_index_in_dim(pairs, self.core, 1, keepdims=False)
        other = lax.dynamic_index_in_dim(pairs, 1 - self.core, 1, keepdims=False)
        halves = mine.astype(F32) + self.swap(other).astype(F32)
        total = lax.dynamic_index_in_dim(halves, self.chip, 0, keepdims=False)
        for k in range(1, self.chips):
            part = lax.dynamic_index_in_dim(halves, (self.chip + k) % self.chips, 0, keepdims=False)
            total = total + self.hop(part.astype(blocks.dtype), k).astype(F32)
        return total


def collect_kernel(blocks, *refs):
    pick_ref, out_ref = refs[0], refs[-1]
    for b in range(blocks):
        block = jnp.concatenate([refs[1 + 2 * b][...], refs[2 + 2 * b][...]], axis=0)
        for e in range(pick_ref.shape[0]):
            out_ref[e, b] = mm(pick_ref[e, b], block).astype(BF16)


def collect(picks, parts):
    local_e, blocks, capacity, rows = picks.shape
    width = 512
    flat = [half for pair in parts for half in pair]
    tile = pl.BlockSpec((rows // 2, width), lambda i: (0, i))
    return pl.pallas_call(
        functools.partial(collect_kernel, blocks),
        grid=(D // width,),
        in_specs=[pl.BlockSpec(picks.shape, lambda i: (0, 0, 0, 0))] + [tile] * len(flat),
        out_specs=pl.BlockSpec((local_e, blocks, capacity, width), lambda i: (0, 0, 0, i)),
        out_shape=jax.ShapeDtypeStruct((local_e, blocks, capacity, D), BF16),
        cost_estimate=pl.CostEstimate(
            flops=2 * local_e * blocks * capacity * rows * D,
            bytes_accessed=2 * blocks * D * (rows + local_e * capacity),
            transcendentals=0,
        ),
        name="collect",
    )(picks, *flat)


def spread_kernel(weight_ref, *refs):
    out_ref = refs[-1]
    total = mm_tn(weight_ref[0], refs[0][...])
    for e in range(1, weight_ref.shape[0]):
        total = total + mm_tn(weight_ref[e], refs[e][...])
    out_ref[...] = total.astype(BF16)


def spread(weights, rows_of):
    local_e, blocks, capacity, rows = weights.shape
    slots = pl.BlockSpec((None, capacity, D), lambda b: (b, 0, 0))
    return pl.pallas_call(
        spread_kernel,
        grid=(blocks,),
        in_specs=[pl.BlockSpec((local_e, None, capacity, rows), lambda b: (0, b, 0, 0))] + [slots] * local_e,
        out_specs=pl.BlockSpec((None, rows, D), lambda b: (b, 0, 0)),
        out_shape=jax.ShapeDtypeStruct((blocks, rows, D), BF16),
        cost_estimate=pl.CostEstimate(
            flops=2 * local_e * blocks * capacity * rows * D,
            bytes_accessed=2 * blocks * D * (rows + local_e * capacity),
            transcendentals=0,
        ),
        name="spread",
    )(weights, *[r.reshape(blocks, capacity, D) for r in rows_of])


def per_device(
    n_grp,
    n_seq,
    tokens,
    cotangent,
    route_ids,
    gain_attn,
    w_query,
    w_key,
    w_value,
    w_out,
    gain_query,
    gain_key,
    gain_ffn,
    router,
    expert_gate,
    expert_up,
    expert_down,
    clip_flags,
    clip_factors,
):
    n_all = n_grp * n_seq
    both = ("grp", "seq")
    rows = tokens.shape[1]
    half = rows // 2
    total = rows * n_seq
    share = D // n_all
    cols = D // n_seq
    local_e = E // n_seq
    capacity = 9 * rows * TOP // (8 * E)
    seq = lax.axis_index("seq")
    ring = Ring(n_seq, n_grp // 2)
    group = Group(n_grp)
    tokens, cotangent, route_ids = tokens[0], cotangent[0], route_ids[0]

    head_scale = jnp.where(clip_flags == 1, jnp.sqrt(clip_factors), jnp.ones_like(clip_factors))
    column_scale = jnp.broadcast_to(head_scale[:, None], (H, HD)).reshape(D)
    clipped_query = (w_query.astype(F32) * column_scale[None, :]).astype(BF16)
    clipped_key = (w_key.astype(F32) * column_scale[None, :]).astype(BF16)

    small = jnp.concatenate(
        [gain_attn[None], gain_query[None], gain_key[None], gain_ffn[None], router.T], axis=0
    ).reshape(1, (4 + E) * share)
    small = lax.all_gather(small, both, axis=0, tiled=True)
    small = small.reshape(n_all, 4 + E, share).transpose(1, 0, 2).reshape(4 + E, D)
    gains = small[:4].astype(F32)
    attn_gain, query_gain, key_gain, ffn_gain = gains[0:1], gains[1:2], gains[2:3], gains[3:4]
    router_t = small[4:]
    query_gain = lax.dynamic_slice(query_gain, (0, seq * cols), (1, cols))
    key_gain = lax.dynamic_slice(key_gain, (0, seq * cols), (1, cols))

    w_qkv = jnp.stack([clipped_query, clipped_key, w_value], axis=1)
    w_qkv = w_qkv.reshape(share, 3, n_seq, cols).transpose(2, 0, 1, 3)
    w_qkv = w_qkv.reshape(n_seq, share, 3 * cols)
    w_got = ring.exchange(lambda t: lax.dynamic_slice(w_qkv, (ring.owners[t], 0, 0), (1, share, 3 * cols)))
    w_part = jnp.zeros_like(w_qkv)
    for t in range(n_seq):
        w_part = lax.dynamic_update_slice(w_part, w_got[t], (ring.owners[t], 0, 0))
    w_qkv = group.gather(w_part.reshape(n_seq * share, 3 * cols)).reshape(D, 3 * cols)

    cosine, sine = rotary_tables(total)

    route_all = lax.all_gather(route_ids, "seq", axis=0, tiled=True).reshape(n_seq, rows, TOP)
    route_all = jnp.take(route_all, ring.owners, axis=0)
    row_at = lax.broadcasted_iota(jnp.int32, (rows, rows), 0)
    col_at = lax.broadcasted_iota(jnp.int32, (rows, rows), 1)
    earlier = (row_at < col_at).astype(BF16)
    slot_at = lax.broadcasted_iota(jnp.int32, (n_seq, capacity, rows), 1)
    picks = []
    for e in range(local_e):
        hit = jnp.any(route_all == seq * local_e + e, axis=-1)
        place = mm(hit.astype(BF16), earlier).astype(jnp.int32)
        picks.append(hit[:, None, :] & (place[:, None, :] == slot_at))
    pick_all = jnp.stack(picks).astype(BF16)

    hidden_in = jnp.zeros((total, D), BF16)
    for t, parts in enumerate(ring.gather(tokens)):
        for i, part in enumerate(parts):
            part = (normalize(part.astype(F32))[0] * attn_gain).astype(BF16)
            hidden_in = lax.dynamic_update_slice(hidden_in, part, (ring.owners[t] * rows + i * half, 0))
    qkv = mm(hidden_in, w_qkv)
    raw_q, raw_k = qkv[:, :cols], qkv[:, cols : 2 * cols]
    sums = jnp.stack([jnp.sum(raw_q * raw_q, axis=-1), jnp.sum(raw_k * raw_k, axis=-1)], axis=0)
    sums = sum(ring.exchange(lambda t: sums))
    query, key, value = prep(qkv, sums.T, query_gain, key_gain, cosine, sine)
    attended_cols, peaks = attention(query, key, value)
    max_logit = lax.all_gather(peaks[:, 0, 0], "seq", axis=0, tiled=True)
    max_logit = lax.pmax(max_logit, "grp")

    cotangent_parts = ring.gather(cotangent)
    grad_slots = collect(pick_all, cotangent_parts)

    attended = lax.all_to_all(attended_cols, "seq", split_axis=0, concat_axis=1, tiled=True)
    w_out_all = lax.all_gather(w_out, both, axis=0, tiled=True)
    inputs = tokens.astype(F32)
    residual_mid = inputs + mm(attended, w_out_all)
    normed_mid, factor_mid = normalize(residual_mid)
    hidden_mid = (normed_mid * ffn_gain).astype(BF16)
    hidden_parts = ring.gather(hidden_mid)
    gate_prob = jax.nn.softmax(mm_nt(hidden_mid, router_t), axis=-1)
    prob_out = gate_prob.T.reshape(n_seq, local_e, rows)
    probs = jnp.stack(
        ring.exchange(lambda t: lax.dynamic_index_in_dim(prob_out, ring.owners[t], 0, keepdims=False))
    )

    gate_w = lax.all_gather(expert_gate, "grp", axis=1, tiled=True)
    up_w = lax.all_gather(expert_up, "grp", axis=1, tiled=True)
    down_w = lax.all_gather(expert_down, "grp", axis=1, tiled=True)

    received_all = collect(pick_all, hidden_parts)
    weighted = [jnp.where(picks[e], probs[:, e][:, None, :], 0.0) for e in range(local_e)]
    slots = n_seq * capacity
    saved, outs = [], []
    for e in range(local_e):
        received = received_all[e].reshape(slots, D)
        gate_val = mm(received, gate_w[e])
        up_val = mm(received, up_w[e])
        sigmoid_gate = jax.nn.sigmoid(gate_val)
        hidden = (gate_val * sigmoid_gate * up_val).astype(BF16)
        outs.append(mm(hidden, down_w[e]).astype(BF16))
        saved.append((received, gate_val, up_val, hidden))
    mixed_out = spread(jnp.stack(weighted).astype(BF16), outs)
    ffn_out = ring.scatter(lambda t: (mixed_out[t, :half], mixed_out[t, half:]))
    block_out = (residual_mid + ffn_out).astype(BF16)

    weight_rows, grad_rows_all, pairs = [], [], []
    for e in range(local_e):
        received, gate_val, up_val, hidden = saved[e]
        sigmoid_gate = jax.nn.sigmoid(gate_val)
        silu_gate = gate_val * sigmoid_gate
        grad_slot = grad_slots[e].reshape(slots, D).astype(F32)
        slot_dot = jnp.sum(grad_slot * outs[e].astype(F32), axis=-1).reshape(n_seq, capacity, 1)
        weight_rows.append(jnp.sum(jnp.where(picks[e], slot_dot, 0.0), axis=1))
        slot_weight = jnp.sum(weighted[e], axis=-1).reshape(slots, 1)
        grad_received = (slot_weight * grad_slot).astype(BF16)
        grad_hidden = mm_nt(grad_received, down_w[e])
        grad_gate = (
            grad_hidden * up_val * sigmoid_gate * (1.0 + gate_val * (1.0 - sigmoid_gate))
        ).astype(BF16)
        grad_up = (grad_hidden * silu_gate).astype(BF16)
        grad_rows_all.append((mm_nt(grad_gate, gate_w[e]) + mm_nt(grad_up, up_w[e])).astype(BF16))
        pairs.append((received, grad_gate, grad_up, hidden, grad_received))

    mixed_grad = spread(pick_all, grad_rows_all)
    grad_hidden_mid = ring.scatter(lambda t: (mixed_grad[t, :half], mixed_grad[t, half:]))
    weight_rows = jnp.stack(weight_rows, axis=1)
    weight_rows = ring.ordered(ring.exchange(lambda t: weight_rows[t]))
    gate_grads = [mm_tn(received, grad_gate).astype(BF16) for received, grad_gate, _, _, _ in pairs]
    up_grads = [mm_tn(received, grad_up).astype(BF16) for received, _, grad_up, _, _ in pairs]
    down_grads = [mm_tn(hidden, grad).astype(BF16) for _, _, _, hidden, grad in pairs]

    grad_prob = weight_rows.reshape(E, rows).T
    grad_logits = gate_prob * (grad_prob - jnp.sum(gate_prob * grad_prob, axis=-1, keepdims=True))
    grad_router = mm_tn(grad_logits, hidden_mid.astype(F32))
    grad_hidden_mid = grad_hidden_mid + mm(grad_logits, router_t.astype(F32))
    grad_ffn_gain = jnp.sum(grad_hidden_mid * normed_mid, axis=0)
    grad_mid = cotangent.astype(F32) + norm_back(grad_hidden_mid * ffn_gain, normed_mid, factor_mid)
    grad_attn = grad_mid.astype(BF16)
    grad_attended = mm_nt(grad_attn, w_out_all).astype(BF16)
    grad_attended = lax.all_to_all(grad_attended, "seq", split_axis=1, concat_axis=0, tiled=True)

    grad_q, grad_k, grad_v = attention_back(query, key, value, grad_attended, cosine, sine)
    factor_q = lax.rsqrt(sums[0] * (1.0 / D) + EPSILON)[:, None]
    factor_k = lax.rsqrt(sums[1] * (1.0 / D) + EPSILON)[:, None]
    normed_q, normed_k = raw_q * factor_q, raw_k * factor_k
    prod_q, prod_k = grad_q * normed_q, grad_k * normed_k
    grad_query_gain = jnp.sum(prod_q, axis=0)
    grad_key_gain = jnp.sum(prod_k, axis=0)
    means = jnp.stack(
        [jnp.sum(prod_q * query_gain, axis=-1), jnp.sum(prod_k * key_gain, axis=-1)], axis=0
    )
    means = sum(ring.exchange(lambda t: means)) * (1.0 / D)
    grad_q = factor_q * (grad_q * query_gain - normed_q * means[0][:, None])
    grad_k = factor_k * (grad_k * key_gain - normed_k * means[1][:, None])
    grad_qkv = jnp.concatenate([grad_q.astype(BF16), grad_k.astype(BF16), grad_v], axis=1)

    grad_in = mm_nt(grad_qkv, w_qkv).astype(BF16)
    grad_hidden_in = ring.scatter(
        lambda t: [
            lax.dynamic_slice(grad_in, (ring.owners[t] * rows + i * half, 0), (half, D)) for i in range(2)
        ]
    )

    grad_w = mm_tn(hidden_in, grad_qkv).astype(BF16)
    grad_w = group.scatter(grad_w.reshape(n_grp, n_seq * share, 3 * cols)).astype(BF16)
    grad_w = grad_w.reshape(n_seq, share, 3 * cols)
    grad_w = ring.ordered(
        ring.exchange(lambda t: lax.dynamic_index_in_dim(grad_w, ring.owners[t], 0, keepdims=False))
    )
    grad_w = grad_w.astype(F32).reshape(n_seq, share, 3, cols).transpose(2, 1, 0, 3)
    grad_w = grad_w.reshape(3, share, D)
    grad_query_w = grad_w[0] * column_scale[None, :]
    grad_key_w = grad_w[1] * column_scale[None, :]
    grad_value_w = grad_w[2]

    grad_attn_all = jnp.zeros((total, D), BF16)
    for t, parts in enumerate(ring.gather(grad_attn)):
        for i, part in enumerate(parts):
            at = (ring.owners[t] * rows + i * half, 0)
            grad_attn_all = lax.dynamic_update_slice(grad_attn_all, part, at)
    grad_out_w = mm_tn(attended_cols, grad_attn_all).astype(BF16)
    grad_out_w = group.scatter(grad_out_w.reshape(n_grp, share, D)).astype(BF16)
    home = [(i * n_seq + j, n_grp * j + i) for j in range(n_seq) for i in range(n_grp)]
    grad_out_w = lax.ppermute(grad_out_w, both, home).astype(F32)

    normed_in, factor_in = normalize(inputs)
    grad_attn_gain = jnp.sum(grad_hidden_in * normed_in, axis=0)
    tokens_grad = grad_mid + norm_back(grad_hidden_in * attn_gain, normed_in, factor_in)

    def place_cols(part):
        return lax.dynamic_update_slice(jnp.zeros((D,), F32), part, (seq * cols,))

    late = jnp.concatenate(
        [
            grad_router,
            grad_ffn_gain[None],
            grad_attn_gain[None],
            place_cols(grad_query_gain)[None],
            place_cols(grad_key_gain)[None],
        ],
        axis=0,
    )
    late = late.reshape(E + 4, n_grp, n_seq, share).transpose(2, 1, 0, 3)
    late = sum(
        ring.exchange(lambda t: lax.dynamic_index_in_dim(late, ring.owners[t], 0, keepdims=False))
    )
    late = group.scatter(late)

    def expert_share(parts):
        summed = lax.psum_scatter(jnp.stack(parts), "grp", scatter_dimension=1, tiled=True)
        return summed.astype(F32)

    return (
        block_out[None],
        tokens_grad[None],
        late[E + 1],
        grad_query_w,
        grad_key_w,
        grad_value_w,
        grad_out_w,
        late[E + 2],
        late[E + 3],
        late[E],
        late[:E].T,
        expert_share(gate_grads),
        expert_share(up_grads),
        expert_share(down_grads),
        max_logit,
        clipped_query,
        clipped_key,
    )


def solution(mesh):
    rows = P("grp", "seq", None)
    vector = P(("grp", "seq"))
    matrix = P(("grp", "seq"), None)
    expert = P("seq", "grp", None)
    return jax.shard_map(
        functools.partial(per_device, mesh.shape["grp"], mesh.shape["seq"]),
        mesh=mesh,
        in_specs=(rows, rows, rows, vector)
        + (matrix,) * 4
        + (vector,) * 3
        + (matrix,)
        + (expert,) * 3
        + (P(), P()),
        out_specs=(rows, rows, vector)
        + (matrix,) * 4
        + (vector,) * 3
        + (matrix,)
        + (expert,) * 3
        + (P(), matrix, matrix),
        check_vma=False,
    )
```
